128 devices in a mesh: tm: 16 (over y, x), orb: 8 (over z, core).
Axes of the slice: x: 4, y: 4, z: 4, core: 2. Of those that a mesh axis runs over, the one named last changes fastest.
Arguments:
- forward: bfloat16 [2, 2, 512, 128, 128], P(None, None, 'tm'), may hold values from -2 to 2
- backward_slab: bfloat16 [2, 2, 512, 128, 128], P(None, None, 'tm', 'orb'), may hold values from -2 to 2
- slot_time: int32 [512], replicated, may hold values from 0 to 511, as said below
- pattern: int32 [128, 128], replicated, may hold values 0 or 1
- coupling: float32 [128, 128], replicated, may hold values from -1 to 1
- hamiltonian: float32 [128, 128], replicated, may hold values from -0.8 to 0.8
- lesser_now: float32 [2, 128, 128], replicated, may hold values from -1.5 to 1.5
Outputs:
- lesser_next: float32 [2, 128, 128], P(None, 'orb')
The draws below stay inside these ranges and needn't reach their ends.
Inputs may be any that keep to these rules, and one draw needn't show every extreme that they name: slot_time is a permutation of the 512 history times. The 32 slots of each index d of tm hold exactly 32 // 16 times of the range [e * 32, (e + 1) * 32) for every index e of tm.
All inputs are finite; a program needn't handle non-finite values.
Results may differ from the reference program's by a relative error of at most 0.0054.
Values may be sent and summed in bfloat16 or wider, within the bound.
No kernel may reach another device: no remote copies, remote signals or barrier semaphores. Data moves between devices by JAX's collectives and lax.ppermute only.
A program may use at most 64 MiB of HBM per device.

```python
import jax
import jax.numpy as jnp
from jax import lax

N = 128
TM_DEV = 32
K = 512
N_TM = 16


def draw_slot_time(key, part):
    per_peer = TM_DEV // N_TM
    first_keys = jax.random.split(jax.random.fold_in(key, 11), N_TM)

    def shuffle_range(one_key):
        return jax.random.permutation(one_key, TM_DEV)
    ranges = jax.vmap(shuffle_range)(first_keys) + (jnp.arange(N_TM) * TM_DEV)[:, None]
    holders = ranges.reshape(N_TM, N_TM, per_peer).transpose(1, 0, 2).reshape(N_TM, TM_DEV)
    second_keys = jax.random.split(jax.random.fold_in(key, 23), N_TM)

    def shuffle_holder(one_key, holder_row):
        return jax.random.permutation(one_key, holder_row)
    shuffled = jax.vmap(shuffle_holder)(second_keys, holders)
    return shuffled.reshape(-1).astype(jnp.int32)


def touch_ends(values, own_key, low, high):
    spot = [jax.random.randint(jax.random.fold_in(own_key, axis), (), 0, length) for axis, length in enumerate(values.shape)]
    longest = values.shape.index(max(values.shape))
    beside = spot[:longest] + [(spot[longest] + 1) % values.shape[longest]] + spot[longest + 1:]
    return values.at[tuple(spot)].set(low).at[tuple(beside)].set(high)


def level_of(rng, dims, cuts, smallest, largest):
    factor_of, own = 1.0, jax.random.fold_in(rng, 6)
    for position, parts in cuts:
        heights = jnp.exp(jax.random.uniform(jax.random.fold_in(own, position), (parts,), jnp.float32, smallest / len(cuts), largest / len(cuts)))
        factor_of = factor_of * jnp.repeat(heights, dims[position] // parts).reshape([-1 if axis == position else 1 for axis in range(len(dims))])
    return factor_of


def centred(rng, dims, deviation, reach, cuts=(), held_as=jnp.bfloat16):
    loudness = level_of(rng, dims, cuts, -0.22, 0.18) if cuts else 1.0
    array = jax.random.normal(rng, dims, jnp.float32) * deviation * loudness
    return jnp.minimum(jnp.maximum(array, -reach), reach).astype(held_as)


def setup_inputs(seed: int = 0) -> dict:
    arg_keys = jax.random.split(jax.random.key(seed), 8)
    return {
        "forward": centred(arg_keys[0], (2, 2, K, N, N), 0.35, 2.0, ((2, 16),)),
        "backward_slab": centred(arg_keys[1], (2, 2, K, N, N), 0.35, 2.0, ((2, 16), (3, 8))),
        "slot_time": draw_slot_time(jax.random.fold_in(arg_keys[7], 71), 0),
        "pattern": touch_ends((jax.random.randint(arg_keys[3], (N, N), 0, 2) < 1).astype(jnp.int32), jax.random.fold_in(arg_keys[3], 1), 0, 1),
        "coupling": centred(arg_keys[4], (N, N), (N // 4) ** -0.5, 1.0, (), jnp.float32),
        "hamiltonian": centred(arg_keys[5], (N, N), 0.1, 0.8, (), jnp.float32),
        "lesser_now": centred(arg_keys[6], (2, N, N), 0.25, 1.5, (), jnp.float32),
    }


history_step = 0.02
update_step = 0.5


def complex_einsum(form, left_re, left_im, right_re, right_im):
    left_re = left_re.astype(jnp.float32)
    left_im = left_im.astype(jnp.float32)
    right_re = right_re.astype(jnp.float32)
    right_im = right_im.astype(jnp.float32)
    real_part = jnp.einsum(form, left_re, right_re) - jnp.einsum(form, left_im, right_im)
    imag_part = jnp.einsum(form, left_re, right_im) + jnp.einsum(form, left_im, right_re)
    return real_part, imag_part


def self_energy(fwd_re, fwd_im, back_re, back_im, interaction):
    fwd_re32 = fwd_re.astype(jnp.float32)
    fwd_im32 = fwd_im.astype(jnp.float32)
    trans_re = jnp.swapaxes(back_re, 1, 2).astype(jnp.float32)
    trans_im = jnp.swapaxes(back_im, 1, 2).astype(jnp.float32)
    bubble_re = (fwd_re32 * trans_re - fwd_im32 * trans_im).astype(jnp.bfloat16)
    bubble_im = (fwd_re32 * trans_im + fwd_im32 * trans_re).astype(jnp.bfloat16)
    inter32 = interaction.astype(jnp.float32)
    left_re = jnp.einsum("ik,skj->sij", inter32, bubble_re.astype(jnp.float32)).astype(jnp.bfloat16)
    left_im = jnp.einsum("ik,skj->sij", inter32, bubble_im.astype(jnp.float32)).astype(jnp.bfloat16)
    screen_re = jnp.einsum("sik,kj->sij", left_re.astype(jnp.float32), inter32)
    screen_im = jnp.einsum("sik,kj->sij", left_im.astype(jnp.float32), inter32)
    direct_re = fwd_re32 * screen_re - fwd_im32 * screen_im
    direct_im = fwd_re32 * screen_im + fwd_im32 * screen_re
    scaled_re = (inter32[None, :, :, None] * fwd_re32[:, None]).astype(jnp.bfloat16)
    scaled_im = (inter32[None, :, :, None] * fwd_im32[:, None]).astype(jnp.bfloat16)
    inner_re, inner_im = complex_einsum("slm,simj->silj", back_re, back_im, scaled_re, scaled_im)
    weighted_re = (inner_re * inter32).astype(jnp.bfloat16)
    weighted_im = (inner_im * inter32).astype(jnp.bfloat16)
    exch_re, exch_im = complex_einsum("sil,silj->sij", fwd_re, fwd_im, weighted_re, weighted_im)
    sigma_re = (direct_re - exch_re).astype(jnp.bfloat16)
    sigma_im = (direct_im - exch_im).astype(jnp.bfloat16)
    return sigma_re, sigma_im


def block_terms(fwd_block, back_block, weights, interaction):
    terms = []
    for branch in (0, 1):
        other = 1 - branch
        sigma_re, sigma_im = self_energy(fwd_block[branch, 0], fwd_block[branch, 1], back_block[other, 0], back_block[other, 1], interaction)
        prod_re, prod_im = complex_einsum("sil,slj->sij", sigma_re, sigma_im, back_block[other, 0], back_block[other, 1])
        terms.append(jnp.stack([prod_re, prod_im]))
    difference = terms[0] - terms[1]
    return jnp.einsum("s,csij->cij", weights, difference)


def reference(forward, backward_slab, slot_time, pattern, coupling, hamiltonian, lesser_now):
    slices_all = forward.shape[2]
    slot_of_time = jnp.argsort(slot_time).astype(jnp.int32)
    backward = jnp.take(backward_slab, slot_of_time, axis=2)
    masked = coupling * pattern.astype(jnp.float32)
    interaction = ((masked + masked.T) * 0.5).astype(jnp.bfloat16)
    time_index = jnp.arange(slices_all, dtype=jnp.int32)
    edges = (time_index == 0) | (time_index == slices_all - 1)
    weights = jnp.where(edges, jnp.float32(0.5), jnp.float32(1.0)) * history_step
    block_count = slices_all // 4
    fwd_blocks = jnp.moveaxis(forward.reshape(2, 2, block_count, 4, N, N), 2, 0)
    back_blocks = jnp.moveaxis(backward.reshape(2, 2, block_count, 4, N, N), 2, 0)
    weight_blocks = weights.reshape(block_count, 4)

    def one_block(inputs):
        return block_terms(inputs[0], inputs[1], inputs[2], interaction)

    terms = lax.map(one_block, (fwd_blocks, back_blocks, weight_blocks))
    collision = jnp.sum(terms, axis=0)
    high = lax.Precision.HIGHEST
    lesser_re = lesser_now[0]
    lesser_im = lesser_now[1]
    comm_re = jnp.dot(hamiltonian, lesser_re, precision=high) - jnp.dot(lesser_re, hamiltonian, precision=high)
    comm_im = jnp.dot(hamiltonian, lesser_im, precision=high) - jnp.dot(lesser_im, hamiltonian, precision=high)
    herm_re = collision[0] + collision[0].T
    herm_im = collision[1] - collision[1].T
    next_re = lesser_re + update_step * (comm_im + herm_im)
    next_im = lesser_im - update_step * (comm_re + herm_re)
    return jnp.stack([next_re, next_im])
```

```python
import jax
import jax.numpy as jnp
from jax import lax
from jax.experimental import pallas as pl
from jax.experimental.pallas import tpu as pltpu
from jax.sharding import PartitionSpec as P

N = 128
bf = jnp.bfloat16
f32 = jnp.float32
HISTORY_STEP = 0.02
UPDATE_STEP = 0.5
UNITS = [(kk, a) for kk in range(4) for a in range(2)]


def rows16(row):
    return jnp.broadcast_to(row, (16, N)).astype(bf)


def cat0(parts):
    return jnp.concatenate(parts, axis=0)


def cat1(parts):
    return jnp.concatenate(parts, axis=1)


def collide(wts, f0, f1, brecv, coup, patt, out, vb, vv, ft, bt, dirt, sig):
    masked = coup[...] * patt[...].astype(f32)
    inter = ((masked + masked.T) * 0.5).astype(bf)
    vv[...] = inter.astype(f32)
    for m in range(N):
        vb[m] = jnp.broadcast_to(vv[:, m:m + 1], (N, N))

    def fmat(kk, a, c):
        return (f0, f1)[kk // 2][kk % 2, a, c]

    def bmat(kk, a, c):
        return cat0([brecv[o, 1 - a, c, kk] for o in range(8)])

    def direct(*accs):
        zero = jnp.zeros((N, N), bf)
        wide = jnp.zeros((N, 2 * N), bf)
        for u, (kk, a) in enumerate(UNITS):
            fr = fmat(kk, a, 0).astype(f32)
            fi = fmat(kk, a, 1).astype(f32)
            tr = bmat(kk, a, 0).T.astype(f32)
            ti = bmat(kk, a, 1).T.astype(f32)
            ft[u, 0] = fr
            ft[u, 1] = fi
            bt[u, 0] = tr
            bt[u, 1] = ti
            bub = cat1([(fr * tr - fi * ti).astype(bf), (fr * ti + fi * tr).astype(bf)])
            stage = (u // 2) % 2
            pltpu.matmul_push_rhs(cat0([bub, wide]), stage, u % 2)
            pltpu.matmul_acc_lhs(accs[u], cat1([inter, zero]), load_staged_rhs=stage)
        both = cat0([cat1([inter, zero]), cat1([zero, inter])])
        for x in range(2):
            pltpu.matmul_push_rhs(both, 0, x)
        lefts = [pltpu.matmul_pop(accs[u]).astype(bf) for u in range(8)]
        for u in range(8):
            pltpu.matmul_acc_lhs(accs[u], lefts[u], load_staged_rhs=0 if u < 2 else None)
        for u in range(8):
            scr = pltpu.matmul_pop(accs[u])
            fr, fi = ft[u, 0], ft[u, 1]
            sr, si = scr[:, :N], scr[:, N:]
            dirt[u, :, :N] = fr * sr - fi * si
            dirt[u, :, N:] = fr * si + fi * sr

    pl.run_scoped(direct, *[pltpu.ACC(u % 2)((N, 2 * N), f32) for u in range(8)])

    def weights(u, m):
        half = []
        for x in range(2):
            fvr = rows16(ft[u, 0, pl.ds(m + x, 1), :])
            fvi = rows16(ft[u, 1, pl.ds(m + x, 1), :])
            v = [vv[16 * i:16 * i + 16].astype(bf) for i in range(8)]
            half.append(cat1([cat0([w * fvr for w in v]), cat0([w * fvi for w in v])]))
        return cat0(half)

    def lhs_rows(u, m):
        re, im = [], []
        for x in range(2):
            bvr = rows16(bt[u, 0, pl.ds(m + x, 1), :])
            bvi = rows16(bt[u, 1, pl.ds(m + x, 1), :])
            pr, pi = [], []
            for i in range(8):
                sl = slice(16 * i, 16 * i + 16)
                a = ft[u, 0, sl].astype(bf)
                b = ft[u, 1, sl].astype(bf)
                v = vb[m + x, sl].astype(bf)
                pr.append((a * bvr - b * bvi) * v)
                pi.append((a * bvi + b * bvr) * v)
            re.append(cat0(pr))
            im.append(cat0(pi))
        return cat1(re), cat1(im)

    def exchange(*flat):
        def acc(u, x, c):
            return flat[4 * (u % 2) + 2 * x + c]

        def step(u, t, last=False):
            for q in range(2):
                base = 8 * t + 4 * q
                lhs = [lhs_rows(u, base + 2 * x) for x in range(2)]
                for x in range(2):
                    pltpu.matmul_acc_lhs(acc(u, x, 0), lhs[x][0], load_staged_rhs=q)
                if not (last and q):
                    for x in range(2):
                        pltpu.matmul_push_rhs(weights(u, base + 4 + 2 * x), 1 - q, x)
                elif u < 7:
                    for x in range(2):
                        pltpu.matmul_push_rhs(weights(u + 1, 2 * x), 0, x)
                for x in range(2):
                    pltpu.matmul_acc_lhs(acc(u, x, 1), lhs[x][1])

        def finish(u):
            rp = pltpu.matmul_pop(acc(u, 0, 0)) + pltpu.matmul_pop(acc(u, 1, 0))
            rq = pltpu.matmul_pop(acc(u, 0, 1)) + pltpu.matmul_pop(acc(u, 1, 1))
            sig[u, :, :N] = (dirt[u, :, :N] - (rp[:, :N] - rq[:, N:])).astype(bf)
            sig[u, :, N:] = (dirt[u, :, N:] - (rp[:, N:] + rq[:, :N])).astype(bf)

        for x in range(2):
            pltpu.matmul_push_rhs(weights(0, 2 * x), 0, x)
        for u in range(8):
            step(u, 0)
            if u:
                finish(u - 1)

            def loop(t, carry):
                step(u, t)
                return carry

            lax.fori_loop(1, N // 8 - 1, loop, 0)
            step(u, N // 8 - 1, True)
        finish(7)

    pl.run_scoped(exchange, *[pltpu.ACC(x)((N, 2 * N), f32) for x in (0, 0, 1, 1, 0, 0, 1, 1)])

    def product(*accs):
        for u, (kk, a) in enumerate(UNITS):
            br = bmat(kk, a, 0)
            bi = bmat(kk, a, 1)
            if a:
                br, bi = -br, -bi
            pltpu.matmul_push_rhs(cat0([cat1([br, bi]), cat1([-bi, br])]), a, kk % 2)
            pltpu.matmul_acc_lhs(accs[kk], sig[u], load_staged_rhs=a)
        total = wts[0] * pltpu.matmul_pop(accs[0])
        for kk in range(1, 4):
            total += wts[kk] * pltpu.matmul_pop(accs[kk])
        re = total[:, :N]
        im = total[:, N:]
        back_re = -0.5 * (re + re.T)
        back_im = 0.5 * (im - im.T)
        for o in range(8):
            out[o, 0] = back_im[16 * o:16 * o + 16]
            out[o, 1] = back_re[16 * o:16 * o + 16]

    pl.run_scoped(product, *[pltpu.ACC(kk % 2)((N, 2 * N), f32) for kk in range(4)])


def shift(orb, half):
    down = 2 * (orb % 2) + half
    return down, (down + orb // 2) % 4


def pack(times, fwd, slab, bsend, f0, f1, wts, seen, sems):
    me = lax.axis_index("tm")
    orb = lax.axis_index("orb")
    down = me // 4
    right = me % 4
    copies = []
    for half, dst in enumerate((f0, f1)):
        dy, dx = shift(orb, half)
        row = (((down + dy) % 4) * 4 + (right + dx) % 4) * 32

        def send(slot, found, dst=dst, half=half, row=row):
            when = times[row + slot]
            mine = when // 32 == me

            @pl.when(mine)
            def _():
                pltpu.make_async_copy(fwd.at[:, :, when % 32], dst.at[found], sems.at[2 * half + found]).start()

            return found + mine.astype(jnp.int32)

        lax.fori_loop(0, 32, send, 0)
        copies += [pltpu.make_async_copy(fwd.at[:, :, 0], dst.at[r], sems.at[2 * half + r]) for r in range(2)]
    for e in range(16):
        seen[e] = 0

    def place(slot, carry):
        when = times[me * 32 + slot]
        holder = when // 32
        rank = seen[holder]
        seen[holder] = rank + 1
        dy = (down - holder // 4 + 4) % 4
        dx = (right - holder % 4 + 4) % 4
        to = ((dx - dy + 4) % 4) * 2 + dy // 2
        spot = (dy % 2) * 2 + rank
        for a in range(2):
            for c in range(2):
                bsend[to, a, c, spot] = slab[a, c, slot]

        @pl.when(to == orb)
        def _():
            edge = jnp.logical_or(when == 0, when == 511)
            wts[spot] = jnp.where(edge, jnp.float32(0.5), jnp.float32(1.0)) * jnp.float32(HISTORY_STEP)

        return carry

    lax.fori_loop(0, 32, place, 0)
    for copy in copies:
        copy.wait()


def on_device(forward, backward_slab, slot_time, pattern, coupling, hamiltonian, lesser_now):
    smem = pl.BlockSpec(memory_space=pltpu.SMEM)
    vmem = pl.BlockSpec(memory_space=pltpu.VMEM)
    shape = jax.ShapeDtypeStruct
    bsend, f0, f1, wts = pl.pallas_call(
        pack,
        out_shape=(shape((8, 2, 2, 4, 16, N), bf), shape((2, 2, 2, N, N), bf), shape((2, 2, 2, N, N), bf),
                   shape((4,), f32)),
        in_specs=[smem, pl.BlockSpec(memory_space=pl.ANY), vmem],
        out_specs=(vmem, vmem, vmem, smem),
        scratch_shapes=[pltpu.SMEM((16,), jnp.int32), pltpu.SemaphoreType.DMA((4,))],
    )(slot_time, forward, backward_slab)
    moved = []
    for half, sent in enumerate((f0, f1)):
        pairs = []
        for e in range(16):
            for o in range(8):
                dy, dx = shift(o, half)
                d = ((e // 4 + dy) % 4) * 4 + (e % 4 + dx) % 4
                pairs.append((e * 8 + o, d * 8 + o))
        moved.append(lax.ppermute(sent, ("tm", "orb"), pairs))
    brecv = lax.all_to_all(bsend, "orb", 0, 0, tiled=True)
    V = pltpu.VMEM
    part = pl.pallas_call(
        collide,
        out_shape=shape((8, 2, 16, N), f32),
        in_specs=[smem] + [vmem] * 5,
        out_specs=vmem,
        scratch_shapes=[V((N, N, N), f32), V((N, N), f32), V((8, 2, N, N), f32), V((8, 2, N, N), f32),
                        V((8, N, 2 * N), f32), V((8, N, 2 * N), bf)],
    )(wts, moved[0], moved[1], brecv, coupling, pattern)
    own = lax.all_to_all(part, "orb", 0, 0, tiled=True).sum(0)
    spread = lax.all_to_all(jnp.broadcast_to(own[None], (16,) + own.shape), "tm", 0, 0, tiled=True)
    start = lax.axis_index("orb") * 16
    high = lax.Precision.HIGHEST
    ham_rows = lax.dynamic_slice_in_dim(hamiltonian, start, 16, 0)
    rows = lax.dynamic_slice_in_dim(lesser_now, start, 16, 1)
    ahead = jnp.dot(ham_rows, jnp.concatenate([lesser_now[0], lesser_now[1]], axis=1), precision=high)
    behind = jnp.dot(rows.reshape(32, N), hamiltonian, precision=high)
    comm_re = ahead[:, :N] - behind[:16]
    comm_im = ahead[:, N:] - behind[16:]
    base = rows + UPDATE_STEP * jnp.stack([comm_im, -comm_re])
    return base + spread.sum(0)


def solution(mesh):
    in_specs = (
        P(None, None, "tm", None, None),
        P(None, None, "tm", "orb", None),
        P(),
        P(),
        P(),
        P(),
        P(),
    )
    run = jax.shard_map(on_device, mesh=mesh, in_specs=in_specs, out_specs=P(None, "orb", None), check_vma=False)
    return run
```

```python
import jax
import jax.numpy as jnp
from jax import lax
from jax.experimental import pallas as pl
from jax.experimental.pallas import tpu as pltpu
from jax.sharding import PartitionSpec as P


N = 128
bf = jnp.bfloat16
f32 = jnp.float32
HISTORY_STEP = 0.02
UPDATE_STEP = 0.5
UNITS = [(kk, a) for kk in range(4) for a in range(2)]


def rows16(row):
    return jnp.broadcast_to(row, (16, N)).astype(bf)


def cat0(parts):
    return jnp.concatenate(parts, axis=0)


def cat1(parts):
    return jnp.concatenate(parts, axis=1)


def collide(wts, f0, f1, brecv, coup, patt, out, vb, vv, ft, bt, dirt, sig):
    masked = coup[...] * patt[...].astype(f32)
    inter = ((masked + masked.T) * 0.5).astype(bf)
    vv[...] = inter.astype(f32)
    for m in range(N):
        vb[m] = jnp.broadcast_to(vv[:, m:m + 1], (N, N))

    def fmat(kk, a, c):
        return (f0, f1)[kk // 2][kk % 2, a, c]

    def bmat(kk, a, c):
        return cat0([brecv[o, 1 - a, c, kk] for o in range(8)])

    def direct(*accs):
        zero = jnp.zeros((N, N), bf)
        wide = jnp.zeros((N, 2 * N), bf)
        for u, (kk, a) in enumerate(UNITS):
            fr = fmat(kk, a, 0).astype(f32)
            fi = fmat(kk, a, 1).astype(f32)
            tr = bmat(kk, a, 0).T.astype(f32)
            ti = bmat(kk, a, 1).T.astype(f32)
            ft[u, 0] = fr
            ft[u, 1] = fi
            bt[u, 0] = tr
            bt[u, 1] = ti
            bub = cat1([(fr * tr - fi * ti).astype(bf), (fr * ti + fi * tr).astype(bf)])
            stage = (u // 2) % 2
            pltpu.matmul_push_rhs(cat0([bub, wide]), stage, u % 2)
            pltpu.matmul_acc_lhs(accs[u], cat1([inter, zero]), load_staged_rhs=stage)
        both = cat0([cat1([inter, zero]), cat1([zero, inter])])
        for x in range(2):
            pltpu.matmul_push_rhs(both, 0, x)
        lefts = [pltpu.matmul_pop(accs[u]).astype(bf) for u in range(8)]
        for u in range(8):
            pltpu.matmul_acc_lhs(accs[u], lefts[u], load_staged_rhs=0 if u < 2 else None)
        for u in range(8):
            scr = pltpu.matmul_pop(accs[u])
            fr, fi = ft[u, 0], ft[u, 1]
            sr, si = scr[:, :N], scr[:, N:]
            dirt[u, :, :N] = fr * sr - fi * si
            dirt[u, :, N:] = fr * si + fi * sr

    pl.run_scoped(direct, *[pltpu.ACC(u % 2)((N, 2 * N), f32) for u in range(8)])

    def weights(u, m):
        half = []
        for x in range(2):
            fvr = rows16(ft[u, 0, pl.ds(m + x, 1), :])
            fvi = rows16(ft[u, 1, pl.ds(m + x, 1), :])
            v = [vv[16 * i:16 * i + 16].astype(bf) for i in range(8)]
            half.append(cat1([cat0([w * fvr for w in v]), cat0([w * fvi for w in v])]))
        return cat0(half)

    def lhs_rows(u, m):
        re, im = [], []
        for x in range(2):
            bvr = rows16(bt[u, 0, pl.ds(m + x, 1), :])
            bvi = rows16(bt[u, 1, pl.ds(m + x, 1), :])
            pr, pi = [], []
            for i in range(8):
                sl = slice(16 * i, 16 * i + 16)
                a = ft[u, 0, sl].astype(bf)
                b = ft[u, 1, sl].astype(bf)
                v = vb[m + x, sl].astype(bf)
                pr.append((a * bvr - b * bvi) * v)
                pi.append((a * bvi + b * bvr) * v)
            re.append(cat0(pr))
            im.append(cat0(pi))
        return cat1(re), cat1(im)

    def exchange(*flat):
        def acc(u, x, c):
            return flat[4 * (u % 2) + 2 * x + c]

        def step(u, t, last=False):
            for q in range(2):
                base = 8 * t + 4 * q
                lhs = [lhs_rows(u, base + 2 * x) for x in range(2)]
                for x in range(2):
                    pltpu.matmul_acc_lhs(acc(u, x, 0), lhs[x][0], load_staged_rhs=q)
                if not (last and q):
                    for x in range(2):
                        pltpu.matmul_push_rhs(weights(u, base + 4 + 2 * x), 1 - q, x)
                elif u < 7:
                    for x in range(2):
                        pltpu.matmul_push_rhs(weights(u + 1, 2 * x), 0, x)
                for x in range(2):
                    pltpu.matmul_acc_lhs(acc(u, x, 1), lhs[x][1])

        def finish(u):
            rp = pltpu.matmul_pop(acc(u, 0, 0)) + pltpu.matmul_pop(acc(u, 1, 0))
            rq = pltpu.matmul_pop(acc(u, 0, 1)) + pltpu.matmul_pop(acc(u, 1, 1))
            sig[u, :, :N] = (dirt[u, :, :N] - (rp[:, :N] - rq[:, N:])).astype(bf)
            sig[u, :, N:] = (dirt[u, :, N:] - (rp[:, N:] + rq[:, :N])).astype(bf)

        for x in range(2):
            pltpu.matmul_push_rhs(weights(0, 2 * x), 0, x)
        for u in range(8):
            step(u, 0)
            if u:
                finish(u - 1)

            def loop(t, carry):
                step(u, t)
                return carry

            lax.fori_loop(1, N // 8 - 1, loop, 0)
            step(u, N // 8 - 1, True)
        finish(7)

    pl.run_scoped(exchange, *[pltpu.ACC(x)((N, 2 * N), f32) for x in (0, 0, 1, 1, 0, 0, 1, 1)])

    def product(*accs):
        for u, (kk, a) in enumerate(UNITS):
            br = bmat(kk, a, 0)
            bi = bmat(kk, a, 1)
            if a:
                br, bi = -br, -bi
            pltpu.matmul_push_rhs(cat0([cat1([br, bi]), cat1([-bi, br])]), a, kk % 2)
            pltpu.matmul_acc_lhs(accs[kk], sig[u], load_staged_rhs=a)
        total = wts[0] * pltpu.matmul_pop(accs[0])
        for kk in range(1, 4):
            total += wts[kk] * pltpu.matmul_pop(accs[kk])
        re = total[:, :N]
        im = total[:, N:]
        back_re = -0.5 * (re + re.T)
        back_im = 0.5 * (im - im.T)
        for o in range(8):
            out[o, 0] = back_im[16 * o:16 * o + 16]
            out[o, 1] = back_re[16 * o:16 * o + 16]

    pl.run_scoped(product, *[pltpu.ACC(kk % 2)((N, 2 * N), f32) for kk in range(4)])


def shift(orb, half):
    down = 2 * (orb & 1) + half
    return down, (down + (orb >> 1)) & 3


def pack(times, fwd, slab, bsend, f0, f1, wts, here, seen, sems):
    me = lax.axis_index("tm")
    orb = lax.axis_index("orb")
    down = me >> 2
    right = me & 3
    rows_in = pltpu.make_async_copy(slab, here, sems.at[4])
    rows_in.start()
    copies = []
    for half, dst in enumerate((f0, f1)):
        dy, dx = shift(orb, half)
        row = ((((down + dy) & 3) << 2) + ((right + dx) & 3)) << 5
        early = jnp.int32(1 << 20)
        late = jnp.int32(-1)
        for slot in range(32):
            when = times[row + slot]
            mine = (when >> 5) == me
            key = slot * 512 + when
            early = jnp.minimum(early, jnp.where(mine, key, 1 << 20))
            late = jnp.maximum(late, jnp.where(mine, key, -1))
        for r, key in enumerate((early, late)):
            copy = pltpu.make_async_copy(fwd.at[:, :, key & 31], dst.at[r], sems.at[2 * half + r])
            copy.start()
            copies.append(copy)
    for e in range(16):
        seen[e] = 0
    rows_in.wait()
    for slot in range(32):
        when = times[(me << 5) + slot]
        holder = when >> 5
        rank = seen[holder]
        seen[holder] = rank + 1
        dy = (down - (holder >> 2)) & 3
        dx = (right - (holder & 3)) & 3
        to = (((dx - dy) & 3) << 1) + (dy >> 1)
        spot = ((dy & 1) << 1) + rank
        for a in range(2):
            for c in range(2):
                bsend[to, a, c, spot] = here[a, c, slot]
        edge = jnp.logical_or(when == 0, when == 511)
        weight = jnp.where(edge, jnp.float32(0.5), jnp.float32(1.0)) * jnp.float32(HISTORY_STEP)
        wts[jnp.where(to == orb, spot, 4)] = weight
    for copy in copies:
        copy.wait()


def on_device(forward, backward_slab, slot_time, pattern, coupling, hamiltonian, lesser_now):
    smem = pl.BlockSpec(memory_space=pltpu.SMEM)
    vmem = pl.BlockSpec(memory_space=pltpu.VMEM)
    hbm = pl.BlockSpec(memory_space=pl.ANY)
    shape = jax.ShapeDtypeStruct
    bsend, f0, f1, wts = pl.pallas_call(
        pack,
        out_shape=(shape((8, 2, 2, 4, 16, N), bf), shape((2, 2, 2, N, N), bf), shape((2, 2, 2, N, N), bf),
                   shape((8,), f32)),
        in_specs=[smem, hbm, hbm],
        out_specs=(vmem, vmem, vmem, smem),
        scratch_shapes=[pltpu.VMEM((2, 2, 32, 16, N), bf), pltpu.SMEM((16,), jnp.int32),
                        pltpu.SemaphoreType.DMA((5,))],
        compiler_params=pltpu.CompilerParams(vmem_limit_bytes=61 << 20),
    )(slot_time, forward, backward_slab)
    moved = []
    for half, sent in enumerate((f0, f1)):
        pairs = []
        for e in range(16):
            for o in range(8):
                dy, dx = shift(o, half)
                d = ((e // 4 + dy) % 4) * 4 + (e % 4 + dx) % 4
                pairs.append((e * 8 + o, d * 8 + o))
        moved.append(lax.ppermute(sent, ("tm", "orb"), pairs))
    brecv = lax.all_to_all(bsend, "orb", 0, 0, tiled=True)
    V = pltpu.VMEM
    part = pl.pallas_call(
        collide,
        out_shape=shape((8, 2, 16, N), f32),
        in_specs=[smem] + [vmem] * 5,
        out_specs=vmem,
        scratch_shapes=[V((N, N, N), f32), V((N, N), f32), V((8, 2, N, N), f32), V((8, 2, N, N), f32),
                        V((8, N, 2 * N), f32), V((8, N, 2 * N), bf)],
        compiler_params=pltpu.CompilerParams(vmem_limit_bytes=24 << 20),
    )(wts, moved[0], moved[1], brecv, coupling, pattern)
    own = lax.all_to_all(part, "orb", 0, 0, tiled=True).sum(0)
    spread = lax.all_to_all(jnp.broadcast_to(own[None], (16,) + own.shape), "tm", 0, 0, tiled=True)
    start = lax.axis_index("orb") * 16
    high = lax.Precision.HIGHEST
    ham_rows = lax.dynamic_slice_in_dim(hamiltonian, start, 16, 0)
    rows = lax.dynamic_slice_in_dim(lesser_now, start, 16, 1)
    ahead = jnp.dot(ham_rows, jnp.concatenate([lesser_now[0], lesser_now[1]], axis=1), precision=high)
    behind = jnp.dot(rows.reshape(32, N), hamiltonian, precision=high)
    comm_re = ahead[:, :N] - behind[:16]
    comm_im = ahead[:, N:] - behind[16:]
    base = rows + UPDATE_STEP * jnp.stack([comm_im, -comm_re])
    return base + spread.sum(0)


def solution(mesh):
    in_specs = (
        P(None, None, "tm", None, None),
        P(None, None, "tm", "orb", None),
        P(),
        P(),
        P(),
        P(),
        P(),
    )
    return jax.shard_map(on_device, mesh=mesh, in_specs=in_specs, out_specs=P(None, "orb", None), check_vma=False)
```

```python
import jax
import jax.numpy as jnp
from jax import lax
from jax.experimental import pallas as pl
from jax.experimental.pallas import tpu as pltpu
from jax.sharding import PartitionSpec as P


N = 128
bf = jnp.bfloat16
f32 = jnp.float32
HISTORY_STEP = 0.02
UPDATE_STEP = 0.5
STEPS = N // 8
UNITS = [(kk, a) for kk in range(4) for a in range(2)]


def rows16(row):
    return jnp.broadcast_to(row, (16, N)).astype(bf)


def cat0(parts):
    return jnp.concatenate(parts, axis=0)


def cat1(parts):
    return jnp.concatenate(parts, axis=1)


def shift(orb, half):
    down = 2 * (orb & 1) + half
    return down, (down + (orb >> 1)) & 3


def matches(times, row, holder):
    early = jnp.int32(1 << 20)
    late = jnp.int32(-1)
    for slot in range(32):
        when = times[row + slot]
        mine = (when >> 5) == holder
        key = slot * 512 + when
        early = jnp.minimum(early, jnp.where(mine, key, 1 << 20))
        late = jnp.maximum(late, jnp.where(mine, key, -1))
    return early & 511, late & 511


def collide(times, f0, f1, brecv, coup, patt, out, vb, vv, ft, bt, dirt, sig):
    masked = coup[...] * patt[...].astype(f32)
    inter = ((masked + masked.T) * 0.5).astype(bf)
    vv[...] = inter.astype(f32)

    def fmat(kk, a, c):
        return (f0, f1)[kk // 2][kk % 2, a, c]

    def bmat(kk, a, c):
        return cat0([brecv[o, 1 - a, c, kk] for o in range(8)])

    def direct(*accs):
        zero = jnp.zeros((N, N), bf)
        wide = jnp.zeros((N, 2 * N), bf)
        for u, (kk, a) in enumerate(UNITS):
            fr = fmat(kk, a, 0).astype(f32)
            fi = fmat(kk, a, 1).astype(f32)
            tr = bmat(kk, a, 0).T.astype(f32)
            ti = bmat(kk, a, 1).T.astype(f32)
            ft[u, 0] = fr
            ft[u, 1] = fi
            bt[u, 0] = tr
            bt[u, 1] = ti
            bub = cat1([(fr * tr - fi * ti).astype(bf), (fr * ti + fi * tr).astype(bf)])
            stage = (u // 2) % 2
            pltpu.matmul_push_rhs(cat0([bub, wide]), stage, u % 2)
            pltpu.matmul_acc_lhs(accs[u], cat1([inter, zero]), load_staged_rhs=stage)
        both = cat0([cat1([inter, zero]), cat1([zero, inter])])
        for x in range(2):
            pltpu.matmul_push_rhs(both, 0, x)
        lefts = [pltpu.matmul_pop(accs[u]).astype(bf) for u in range(8)]
        for u in range(8):
            pltpu.matmul_acc_lhs(accs[u], lefts[u], load_staged_rhs=0 if u < 2 else None)
        for u in range(8):
            scr = pltpu.matmul_pop(accs[u])
            fr, fi = ft[u, 0], ft[u, 1]
            sr, si = scr[:, :N], scr[:, N:]
            dirt[u, :, :N] = fr * sr - fi * si
            dirt[u, :, N:] = fr * si + fi * sr

    pl.run_scoped(direct, *[pltpu.ACC(u % 2)((N, 2 * N), f32) for u in range(8)])

    def weights(u, m):
        half = []
        for x in range(2):
            fvr = rows16(ft[u, 0, pl.ds(m + x, 1), :])
            fvi = rows16(ft[u, 1, pl.ds(m + x, 1), :])
            v = [vv[16 * i:16 * i + 16].astype(bf) for i in range(8)]
            half.append(cat1([cat0([w * fvr for w in v]), cat0([w * fvi for w in v])]))
        return cat0(half)

    def lhs_rows(u, m, first):
        re, im = [], []
        for x in range(2):
            bvr = rows16(bt[u, 0, pl.ds(m + x, 1), :])
            bvi = rows16(bt[u, 1, pl.ds(m + x, 1), :])
            pr, pi = [], []
            for i in range(8):
                sl = slice(16 * i, 16 * i + 16)
                a = ft[u, 0, sl].astype(bf)
                b = ft[u, 1, sl].astype(bf)
                if first:
                    wide = jnp.broadcast_to(vv[sl, m + x:m + x + 1], (16, N))
                    vb[m + x, sl] = wide
                else:
                    wide = vb[m + x, sl]
                v = wide.astype(bf)
                pr.append((a * bvr - b * bvi) * v)
                pi.append((a * bvi + b * bvr) * v)
            re.append(cat0(pr))
            im.append(cat0(pi))
        return cat1(re), cat1(im)

    def exchange(*flat):
        def step(u, par, t, first=False, last=False):
            acc = flat[4 * par:4 * par + 4]
            for q in range(2):
                base = 8 * t + 4 * q
                lhs = [lhs_rows(u, base + 2 * x, first) for x in range(2)]
                for x in range(2):
                    pltpu.matmul_acc_lhs(acc[2 * x], lhs[x][0], load_staged_rhs=q)
                if not (last and q):
                    for x in range(2):
                        pltpu.matmul_push_rhs(weights(u, base + 4 + 2 * x), 1 - q, x)
                elif not (isinstance(u, int) and u == 7):
                    for x in range(2):
                        pltpu.matmul_push_rhs(weights(u + 1, 2 * x), 0, x)
                for x in range(2):
                    pltpu.matmul_acc_lhs(acc[2 * x + 1], lhs[x][1])

        def finish(u, par):
            acc = flat[4 * par:4 * par + 4]
            rp = pltpu.matmul_pop(acc[0]) + pltpu.matmul_pop(acc[2])
            rq = pltpu.matmul_pop(acc[1]) + pltpu.matmul_pop(acc[3])
            sig[u, :, :N] = (dirt[u, :, :N] - (rp[:, :N] - rq[:, N:])).astype(bf)
            sig[u, :, N:] = (dirt[u, :, N:] - (rp[:, N:] + rq[:, :N])).astype(bf)

        def unit(u, par):
            step(u, par, 0)
            finish(u - 1, 1 - par)

            def loop(t, inner):
                step(u, par, t)
                return inner

            lax.fori_loop(1, STEPS - 1, loop, 0, unroll=7)
            step(u, par, STEPS - 1, last=True)

        def pair(p, carry):
            unit(2 * p + 1, 1)
            unit(2 * p + 2, 0)
            return carry

        for x in range(2):
            pltpu.matmul_push_rhs(weights(0, 2 * x), 0, x)
        for t in range(STEPS):
            step(0, 0, t, first=True, last=t == STEPS - 1)
        lax.fori_loop(0, 3, pair, 0)
        unit(7, 1)
        finish(7, 1)

    pl.run_scoped(exchange, *[pltpu.ACC(x)((N, 2 * N), f32) for x in (0, 0, 1, 1, 0, 0, 1, 1)])

    def product(*accs):
        for u, (kk, a) in enumerate(UNITS):
            br = bmat(kk, a, 0)
            bi = bmat(kk, a, 1)
            if a:
                br, bi = -br, -bi
            pltpu.matmul_push_rhs(cat0([cat1([br, bi]), cat1([-bi, br])]), a, kk % 2)
            pltpu.matmul_acc_lhs(accs[kk], sig[u], load_staged_rhs=a)
        me = lax.axis_index("tm")
        wts = []
        for half in range(2):
            dy, dx = shift(lax.axis_index("orb"), half)
            holder = ((((me >> 2) - dy) & 3) << 2) + (((me & 3) - dx) & 3)
            for when in matches(times, me << 5, holder):
                edge = jnp.logical_or(when == 0, when == 511)
                wts.append(jnp.where(edge, jnp.float32(0.5), jnp.float32(1.0)) * jnp.float32(HISTORY_STEP))
        total = wts[0] * pltpu.matmul_pop(accs[0])
        for kk in range(1, 4):
            total += wts[kk] * pltpu.matmul_pop(accs[kk])
        re = total[:, :N]
        im = total[:, N:]
        back_re = -0.5 * (re + re.T)
        back_im = 0.5 * (im - im.T)
        for o in range(8):
            out[o, 0] = back_im[16 * o:16 * o + 16]
            out[o, 1] = back_re[16 * o:16 * o + 16]

    pl.run_scoped(product, *[pltpu.ACC(kk % 2)((N, 2 * N), f32) for kk in range(4)])


def pack(times, fwd, slab, bsend, f0, f1, here, seen, sems):
    me = lax.axis_index("tm")
    orb = lax.axis_index("orb")
    down = me >> 2
    right = me & 3
    rows_in = pltpu.make_async_copy(slab, here, sems.at[4])
    rows_in.start()
    copies = []
    for half, dst in enumerate((f0, f1)):
        dy, dx = shift(orb, half)
        row = ((((down + dy) & 3) << 2) + ((right + dx) & 3)) << 5
        for r, when in enumerate(matches(times, row, me)):
            copy = pltpu.make_async_copy(fwd.at[:, :, when & 31], dst.at[r], sems.at[2 * half + r])
            copy.start()
            copies.append(copy)
    for e in range(16):
        seen[e] = 0
    rows_in.wait()
    for slot in range(32):
        when = times[(me << 5) + slot]
        holder = when >> 5
        rank = seen[holder]
        seen[holder] = rank + 1
        dy = (down - (holder >> 2)) & 3
        dx = (right - (holder & 3)) & 3
        to = (((dx - dy) & 3) << 1) + (dy >> 1)
        spot = ((dy & 1) << 1) + rank
        for a in range(2):
            for c in range(2):
                bsend[to, a, c, spot] = here[a, c, slot]
    for copy in copies:
        copy.wait()


def on_device(forward, backward_slab, slot_time, pattern, coupling, hamiltonian, lesser_now):
    smem = pl.BlockSpec(memory_space=pltpu.SMEM)
    vmem = pl.BlockSpec(memory_space=pltpu.VMEM)
    hbm = pl.BlockSpec(memory_space=pl.ANY)
    shape = jax.ShapeDtypeStruct
    bsend, f0, f1 = pl.pallas_call(
        pack,
        out_shape=(shape((8, 2, 2, 4, 16, N), bf), shape((2, 2, 2, N, N), bf), shape((2, 2, 2, N, N), bf)),
        in_specs=[smem, hbm, hbm],
        out_specs=(vmem, vmem, vmem),
        scratch_shapes=[pltpu.VMEM((2, 2, 32, 16, N), bf), pltpu.SMEM((16,), jnp.int32),
                        pltpu.SemaphoreType.DMA((5,))],
        compiler_params=pltpu.CompilerParams(vmem_limit_bytes=61 << 20),
    )(slot_time, forward, backward_slab)
    moved = []
    for half, sent in enumerate((f0, f1)):
        pairs = []
        for e in range(16):
            for o in range(8):
                dy, dx = shift(o, half)
                d = ((e // 4 + dy) % 4) * 4 + (e % 4 + dx) % 4
                pairs.append((e * 8 + o, d * 8 + o))
        moved.append(lax.ppermute(sent, ("tm", "orb"), pairs))
    brecv = lax.all_to_all(bsend, "orb", 0, 0, tiled=True)
    V = pltpu.VMEM
    part = pl.pallas_call(
        collide,
        out_shape=shape((8, 2, 16, N), f32),
        in_specs=[smem] + [vmem] * 5,
        out_specs=vmem,
        scratch_shapes=[V((N, N, N), f32), V((N, N), f32), V((8, 2, N, N), f32), V((8, 2, N, N), f32),
                        V((8, N, 2 * N), f32), V((8, N, 2 * N), bf)],
        compiler_params=pltpu.CompilerParams(vmem_limit_bytes=24 << 20),
    )(slot_time, moved[0], moved[1], brecv, coupling, pattern)
    own = lax.all_to_all(part, "orb", 0, 0, tiled=True).sum(0)
    spread = lax.all_to_all(jnp.broadcast_to(own[None], (16,) + own.shape), "tm", 0, 0, tiled=True)
    start = lax.axis_index("orb") * 16
    high = lax.Precision.HIGHEST
    ham_rows = lax.dynamic_slice_in_dim(hamiltonian, start, 16, 0)
    rows = lax.dynamic_slice_in_dim(lesser_now, start, 16, 1)
    ahead = jnp.dot(ham_rows, jnp.concatenate([lesser_now[0], lesser_now[1]], axis=1), precision=high)
    behind = jnp.dot(rows.reshape(32, N), hamiltonian, precision=high)
    comm_re = ahead[:, :N] - behind[:16]
    comm_im = ahead[:, N:] - behind[16:]
    base = rows + UPDATE_STEP * jnp.stack([comm_im, -comm_re])
    return base + spread.sum(0)


def solution(mesh):
    in_specs = (
        P(None, None, "tm", None, None),
        P(None, None, "tm", "orb", None),
        P(),
        P(),
        P(),
        P(),
        P(),
    )
    return jax.shard_map(on_device, mesh=mesh, in_specs=in_specs, out_specs=P(None, "orb", None), check_vma=False)
```

```python
import jax
import jax.numpy as jnp
from jax import lax
from jax.experimental import pallas as pl
from jax.experimental.pallas import tpu as pltpu
from jax.sharding import PartitionSpec as P


N = 128
bf = jnp.bfloat16
f32 = jnp.float32
HISTORY_STEP = 0.02
UPDATE_STEP = 0.5
STEPS = N // 8
UNITS = [(kk, a) for kk in range(4) for a in range(2)]


def rows16(row):
    return jnp.broadcast_to(row, (16, N)).astype(bf)


def cat0(parts):
    return jnp.concatenate(parts, axis=0)


def cat1(parts):
    return jnp.concatenate(parts, axis=1)


def shift(orb, half):
    down = 2 * (orb & 1) + half
    return down, (down + (orb >> 1)) & 3


def matches(times, row, holder):
    early = jnp.int32(1 << 20)
    late = jnp.int32(-1)
    for slot in range(32):
        when = times[row + slot]
        mine = (when >> 5) == holder
        key = slot * 512 + when
        early = jnp.minimum(early, jnp.where(mine, key, 1 << 20))
        late = jnp.maximum(late, jnp.where(mine, key, -1))
    return early & 511, late & 511


def collide(times, f0, f1, brecv, coup, patt, out, vb, vv, ft, bt, dirt, sig, wts):
    masked = coup[...] * patt[...].astype(f32)
    inter = ((masked + masked.T) * 0.5).astype(bf)
    vv[...] = inter.astype(f32)

    def fmat(kk, a, c):
        return (f0, f1)[kk // 2][kk % 2, a, c]

    def bmat(kk, a, c):
        return cat0([brecv[o, 1 - a, c, kk] for o in range(8)])

    def direct(*accs):
        me = lax.axis_index("tm")
        for half in range(2):
            dy, dx = shift(lax.axis_index("orb"), half)
            holder = ((((me >> 2) - dy) & 3) << 2) + (((me & 3) - dx) & 3)
            for r, when in enumerate(matches(times, me << 5, holder)):
                edge = jnp.logical_or(when == 0, when == 511)
                weight = jnp.where(edge, jnp.float32(0.5), jnp.float32(1.0)) * jnp.float32(HISTORY_STEP)
                wts[2 * half + r] = weight
        zero = jnp.zeros((N, N), bf)
        wide = jnp.zeros((N, 2 * N), bf)
        for u, (kk, a) in enumerate(UNITS):
            fr = fmat(kk, a, 0).astype(f32)
            fi = fmat(kk, a, 1).astype(f32)
            tr = bmat(kk, a, 0).T.astype(f32)
            ti = bmat(kk, a, 1).T.astype(f32)
            ft[u, 0] = fr
            ft[u, 1] = fi
            bt[u, 0] = tr
            bt[u, 1] = ti
            bub = cat1([(fr * tr - fi * ti).astype(bf), (fr * ti + fi * tr).astype(bf)])
            stage = (u // 2) % 2
            pltpu.matmul_push_rhs(cat0([bub, wide]), stage, u % 2)
            pltpu.matmul_acc_lhs(accs[u], cat1([inter, zero]), load_staged_rhs=stage)
        both = cat0([cat1([inter, zero]), cat1([zero, inter])])
        for x in range(2):
            pltpu.matmul_push_rhs(both, 0, x)
        lefts = [pltpu.matmul_pop(accs[u]).astype(bf) for u in range(8)]
        for u in range(8):
            pltpu.matmul_acc_lhs(accs[u], lefts[u], load_staged_rhs=0 if u < 2 else None)
        for u in range(8):
            scr = pltpu.matmul_pop(accs[u])
            fr, fi = ft[u, 0], ft[u, 1]
            sr, si = scr[:, :N], scr[:, N:]
            dirt[u, :, :N] = fr * sr - fi * si
            dirt[u, :, N:] = fr * si + fi * sr

    pl.run_scoped(direct, *[pltpu.ACC(u % 2)((N, 2 * N), f32) for u in range(8)])

    def weights(u, m):
        half = []
        for x in range(2):
            fvr = rows16(ft[u, 0, pl.ds(m + x, 1), :])
            fvi = rows16(ft[u, 1, pl.ds(m + x, 1), :])
            v = [vv[16 * i:16 * i + 16].astype(bf) for i in range(8)]
            half.append(cat1([cat0([w * fvr for w in v]), cat0([w * fvi for w in v])]))
        return cat0(half)

    def lhs_rows(u, m, first):
        re, im = [], []
        for x in range(2):
            bvr = rows16(bt[u, 0, pl.ds(m + x, 1), :])
            bvi = rows16(bt[u, 1, pl.ds(m + x, 1), :])
            pr, pi = [], []
            for i in range(8):
                sl = slice(16 * i, 16 * i + 16)
                a = ft[u, 0, sl].astype(bf)
                b = ft[u, 1, sl].astype(bf)
                if first:
                    wide = jnp.broadcast_to(vv[sl, m + x:m + x + 1], (16, N))
                    vb[m + x, sl] = wide
                else:
                    wide = vb[m + x, sl]
                v = wide.astype(bf)
                pr.append((a * bvr - b * bvi) * v)
                pi.append((a * bvi + b * bvr) * v)
            re.append(cat0(pr))
            im.append(cat0(pi))
        return cat1(re), cat1(im)

    def exchange(*flat):
        def step(u, par, t, first=False, last=False):
            acc = flat[4 * par:4 * par + 4]
            for q in range(2):
                base = 8 * t + 4 * q
                lhs = [lhs_rows(u, base + 2 * x, first) for x in range(2)]
                for x in range(2):
                    pltpu.matmul_acc_lhs(acc[2 * x], lhs[x][0], load_staged_rhs=q)
                if not (last and q):
                    for x in range(2):
                        pltpu.matmul_push_rhs(weights(u, base + 4 + 2 * x), 1 - q, x)
                elif not (isinstance(u, int) and u == 7):
                    for x in range(2):
                        pltpu.matmul_push_rhs(weights(u + 1, 2 * x), 0, x)
                for x in range(2):
                    pltpu.matmul_acc_lhs(acc[2 * x + 1], lhs[x][1])

        def finish(u, par):
            acc = flat[4 * par:4 * par + 4]
            rp = pltpu.matmul_pop(acc[0]) + pltpu.matmul_pop(acc[2])
            rq = pltpu.matmul_pop(acc[1]) + pltpu.matmul_pop(acc[3])
            sig[u, :, :N] = (dirt[u, :, :N] - (rp[:, :N] - rq[:, N:])).astype(bf)
            sig[u, :, N:] = (dirt[u, :, N:] - (rp[:, N:] + rq[:, :N])).astype(bf)

        def unit(u, par):
            step(u, par, 0)
            finish(u - 1, 1 - par)

            def loop(t, inner):
                step(u, par, t)
                return inner

            lax.fori_loop(1, STEPS - 1, loop, 0, unroll=7)
            step(u, par, STEPS - 1, last=True)

        def pair(p, carry):
            unit(2 * p + 1, 1)
            unit(2 * p + 2, 0)
            return carry

        for x in range(2):
            pltpu.matmul_push_rhs(weights(0, 2 * x), 0, x)
        for t in range(STEPS):
            step(0, 0, t, first=True, last=t == STEPS - 1)
        lax.fori_loop(0, 3, pair, 0)
        unit(7, 1)
        finish(7, 1)

    pl.run_scoped(exchange, *[pltpu.ACC(x)((N, 2 * N), f32) for x in (0, 0, 1, 1, 0, 0, 1, 1)])

    def product(*accs):
        for u, (kk, a) in enumerate(UNITS):
            br = bmat(kk, a, 0)
            bi = bmat(kk, a, 1)
            if a:
                br, bi = -br, -bi
            pltpu.matmul_push_rhs(cat0([cat1([br, bi]), cat1([-bi, br])]), a, kk % 2)
            pltpu.matmul_acc_lhs(accs[kk], sig[u], load_staged_rhs=a)
        total = wts[0] * pltpu.matmul_pop(accs[0])
        for kk in range(1, 4):
            total += wts[kk] * pltpu.matmul_pop(accs[kk])
        re = total[:, :N]
        im = total[:, N:]
        back_re = -0.5 * (re + re.T)
        back_im = 0.5 * (im - im.T)
        for o in range(8):
            out[o, 0] = back_im[16 * o:16 * o + 16]
            out[o, 1] = back_re[16 * o:16 * o + 16]

    pl.run_scoped(product, *[pltpu.ACC(kk % 2)((N, 2 * N), f32) for kk in range(4)])


def pack(times, fwd, slab, bsend, f0, f1, here, placed, slices, seen, sems):
    me = lax.axis_index("tm")
    orb = lax.axis_index("orb")
    down = me >> 2
    right = me & 3
    rows_in = pltpu.make_async_copy(slab, here, sems.at[4])
    rows_in.start()
    copies = []
    for half, dst in enumerate((f0, f1)):
        dy, dx = shift(orb, half)
        row = ((((down + dy) & 3) << 2) + ((right + dx) & 3)) << 5
        for r, when in enumerate(matches(times, row, me)):
            spot = 2 * half + r
            copy = pltpu.make_async_copy(fwd.at[:, :, when & 31], slices.at[spot], sems.at[spot])
            copy.start()
            copies.append((copy, pltpu.make_async_copy(slices.at[spot], dst.at[r], sems.at[6 + spot])))
    for e in range(16):
        seen[e] = 0
    rows_in.wait()
    for slot in range(32):
        when = times[(me << 5) + slot]
        holder = when >> 5
        rank = seen[holder]
        seen[holder] = rank + 1
        dy = (down - (holder >> 2)) & 3
        dx = (right - (holder & 3)) & 3
        to = (((dx - dy) & 3) << 1) + (dy >> 1)
        spot = ((dy & 1) << 1) + rank
        for a in range(2):
            for c in range(2):
                placed[to, a, c, spot] = here[a, c, slot]
    for copy, onward in copies:
        copy.wait()
        onward.start()
    rows_out = pltpu.make_async_copy(placed, bsend, sems.at[5])
    rows_out.start()
    for copy, onward in copies:
        onward.wait()
    rows_out.wait()


def on_device(forward, backward_slab, slot_time, pattern, coupling, hamiltonian, lesser_now):
    smem = pl.BlockSpec(memory_space=pltpu.SMEM)
    vmem = pl.BlockSpec(memory_space=pltpu.VMEM)
    hbm = pl.BlockSpec(memory_space=pl.ANY)
    shape = jax.ShapeDtypeStruct
    bsend, f0, f1 = pl.pallas_call(
        pack,
        out_shape=(shape((8, 2, 2, 4, 16, N), bf), shape((2, 2, 2, N, N), bf), shape((2, 2, 2, N, N), bf)),
        in_specs=[smem, hbm, hbm],
        out_specs=(hbm, hbm, hbm),
        scratch_shapes=[pltpu.VMEM((2, 2, 32, 16, N), bf), pltpu.VMEM((8, 2, 2, 4, 16, N), bf),
                        pltpu.VMEM((4, 2, 2, N, N), bf), pltpu.SMEM((16,), jnp.int32),
                        pltpu.SemaphoreType.DMA((10,))],
        compiler_params=pltpu.CompilerParams(vmem_limit_bytes=61 << 20),
    )(slot_time, forward, backward_slab)
    moved = []
    for half, sent in enumerate((f0, f1)):
        pairs = []
        for e in range(16):
            for o in range(8):
                dy, dx = shift(o, half)
                d = ((e // 4 + dy) % 4) * 4 + (e % 4 + dx) % 4
                pairs.append((e * 8 + o, d * 8 + o))
        moved.append(lax.ppermute(sent, ("tm", "orb"), pairs))
    brecv = lax.all_to_all(bsend, "orb", 0, 0, tiled=True)
    V = pltpu.VMEM
    part = pl.pallas_call(
        collide,
        out_shape=shape((8, 2, 16, N), f32),
        in_specs=[smem] + [vmem] * 5,
        out_specs=vmem,
        scratch_shapes=[V((N, N, N), f32), V((N, N), f32), V((8, 2, N, N), f32), V((8, 2, N, N), f32),
                        V((8, N, 2 * N), f32), V((8, N, 2 * N), bf), pltpu.SMEM((4,), f32)],
        compiler_params=pltpu.CompilerParams(vmem_limit_bytes=24 << 20),
    )(slot_time, moved[0], moved[1], brecv, coupling, pattern)
    own = lax.all_to_all(part, "orb", 0, 0, tiled=True).sum(0)
    copies = jnp.broadcast_to(own.astype(bf)[None], (16,) + own.shape)
    spread = lax.all_to_all(copies, "tm", 0, 0, tiled=True).astype(f32)
    start = lax.axis_index("orb") * 16
    high = lax.Precision.HIGHEST
    ham_rows = lax.dynamic_slice_in_dim(hamiltonian, start, 16, 0)
    rows = lax.dynamic_slice_in_dim(lesser_now, start, 16, 1)
    ahead = jnp.dot(ham_rows, jnp.concatenate([lesser_now[0], lesser_now[1]], axis=1), precision=high)
    behind = jnp.dot(rows.reshape(32, N), hamiltonian, precision=high)
    comm_re = ahead[:, :N] - behind[:16]
    comm_im = ahead[:, N:] - behind[16:]
    base = rows + UPDATE_STEP * jnp.stack([comm_im, -comm_re])
    return base + spread.sum(0)


def solution(mesh):
    in_specs = (
        P(None, None, "tm", None, None),
        P(None, None, "tm", "orb", None),
        P(),
        P(),
        P(),
        P(),
        P(),
    )
    return jax.shard_map(on_device, mesh=mesh, in_specs=in_specs, out_specs=P(None, "orb", None), check_vma=False)
```

```python
import jax
import jax.numpy as jnp
from jax import lax
from jax.experimental import pallas as pl
from jax.experimental.pallas import tpu as pltpu
from jax.sharding import PartitionSpec as P


N = 128
bf = jnp.bfloat16
f32 = jnp.float32
HISTORY_STEP = 0.02
UPDATE_STEP = 0.5
STEPS = N // 8
UNITS = [(kk, a) for kk in range(4) for a in range(2)]


def rows16(row):
    return jnp.broadcast_to(row, (16, N)).astype(bf)


def cat0(parts):
    return jnp.concatenate(parts, axis=0)


def cat1(parts):
    return jnp.concatenate(parts, axis=1)


def shift(orb, half):
    down = 2 * (orb & 1) + half
    return down, (down + (orb >> 1)) & 3


def matches(times, row, holder):
    early = jnp.int32(1 << 20)
    late = jnp.int32(-1)
    for slot in range(32):
        when = times[row + slot]
        mine = (when >> 5) == holder
        key = slot * 512 + when
        early = jnp.minimum(early, jnp.where(mine, key, 1 << 20))
        late = jnp.maximum(late, jnp.where(mine, key, -1))
    return early & 511, late & 511


def collide(times, f0, f1, brecv, coup, patt, out, vb, vv, ft, bt, dirt, sig, wts):
    masked = coup[...] * patt[...].astype(f32)
    inter = ((masked + masked.T) * 0.5).astype(bf)
    vv[...] = inter.astype(f32)

    def fmat(kk, a, c):
        return (f0, f1)[kk // 2][kk % 2, a, c]

    def bmat(kk, a, c):
        return cat0([brecv[o, 1 - a, c, kk] for o in range(8)])

    def direct(*accs):
        me = lax.axis_index("tm")
        for half in range(2):
            dy, dx = shift(lax.axis_index("orb"), half)
            holder = ((((me >> 2) - dy) & 3) << 2) + (((me & 3) - dx) & 3)
            for r, when in enumerate(matches(times, me << 5, holder)):
                edge = jnp.logical_or(when == 0, when == 511)
                weight = jnp.where(edge, jnp.float32(0.5), jnp.float32(1.0)) * jnp.float32(HISTORY_STEP)
                wts[2 * half + r] = weight
        zero = jnp.zeros((N, N), bf)
        wide = jnp.zeros((N, 2 * N), bf)
        for u, (kk, a) in enumerate(UNITS):
            fr = fmat(kk, a, 0).astype(f32)
            fi = fmat(kk, a, 1).astype(f32)
            tr = bmat(kk, a, 0).T.astype(f32)
            ti = bmat(kk, a, 1).T.astype(f32)
            ft[u, 0] = fr
            ft[u, 1] = fi
            bt[u, 0] = tr
            bt[u, 1] = ti
            bub = cat1([(fr * tr - fi * ti).astype(bf), (fr * ti + fi * tr).astype(bf)])
            stage = (u // 2) % 2
            pltpu.matmul_push_rhs(cat0([bub, wide]), stage, u % 2)
            pltpu.matmul_acc_lhs(accs[u], cat1([inter, zero]), load_staged_rhs=stage)
        both = cat0([cat1([inter, zero]), cat1([zero, inter])])
        for x in range(2):
            pltpu.matmul_push_rhs(both, 0, x)
        lefts = [pltpu.matmul_pop(accs[u]).astype(bf) for u in range(8)]
        for u in range(8):
            pltpu.matmul_acc_lhs(accs[u], lefts[u], load_staged_rhs=0 if u < 2 else None)
        for u in range(8):
            scr = pltpu.matmul_pop(accs[u])
            fr, fi = ft[u, 0], ft[u, 1]
            sr, si = scr[:, :N], scr[:, N:]
            dirt[u, :, :N] = fr * sr - fi * si
            dirt[u, :, N:] = fr * si + fi * sr

    pl.run_scoped(direct, *[pltpu.ACC(u % 2)((N, 2 * N), f32) for u in range(8)])

    def weights(u, m):
        half = []
        for x in range(2):
            fvr = rows16(ft[u, 0, pl.ds(m + x, 1), :])
            fvi = rows16(ft[u, 1, pl.ds(m + x, 1), :])
            v = [vv[16 * i:16 * i + 16].astype(bf) for i in range(8)]
            half.append(cat1([cat0([w * fvr for w in v]), cat0([w * fvi for w in v])]))
        return cat0(half)

    def lhs_rows(u, m, first):
        re, im = [], []
        for x in range(2):
            bvr = rows16(bt[u, 0, pl.ds(m + x, 1), :])
            bvi = rows16(bt[u, 1, pl.ds(m + x, 1), :])
            pr, pi = [], []
            for i in range(8):
                sl = slice(16 * i, 16 * i + 16)
                a = ft[u, 0, sl].astype(bf)
                b = ft[u, 1, sl].astype(bf)
                if first:
                    wide = jnp.broadcast_to(vv[sl, m + x:m + x + 1], (16, N))
                    vb[m + x, sl] = wide
                else:
                    wide = vb[m + x, sl]
                v = wide.astype(bf)
                pr.append((a * bvr - b * bvi) * v)
                pi.append((a * bvi + b * bvr) * v)
            re.append(cat0(pr))
            im.append(cat0(pi))
        return cat1(re), cat1(im)

    def exchange(*flat):
        def step(u, par, t, first=False, last=False):
            acc = flat[4 * par:4 * par + 4]
            for q in range(2):
                base = 8 * t + 4 * q
                lhs = [lhs_rows(u, base + 2 * x, first) for x in range(2)]
                for x in range(2):
                    pltpu.matmul_acc_lhs(acc[2 * x], lhs[x][0], load_staged_rhs=q)
                if not (last and q):
                    for x in range(2):
                        pltpu.matmul_push_rhs(weights(u, base + 4 + 2 * x), 1 - q, x)
                elif not (isinstance(u, int) and u == 7):
                    for x in range(2):
                        pltpu.matmul_push_rhs(weights(u + 1, 2 * x), 0, x)
                for x in range(2):
                    pltpu.matmul_acc_lhs(acc[2 * x + 1], lhs[x][1])

        def finish(u, par):
            acc = flat[4 * par:4 * par + 4]
            rp = pltpu.matmul_pop(acc[0]) + pltpu.matmul_pop(acc[2])
            rq = pltpu.matmul_pop(acc[1]) + pltpu.matmul_pop(acc[3])
            sig[u, :, :N] = (dirt[u, :, :N] - (rp[:, :N] - rq[:, N:])).astype(bf)
            sig[u, :, N:] = (dirt[u, :, N:] - (rp[:, N:] + rq[:, :N])).astype(bf)

        def unit(u, par):
            step(u, par, 0)
            finish(u - 1, 1 - par)

            def loop(t, inner):
                step(u, par, t)
                return inner

            lax.fori_loop(1, STEPS - 1, loop, 0, unroll=7)
            step(u, par, STEPS - 1, last=True)

        def pair(p, carry):
            unit(2 * p + 1, 1)
            unit(2 * p + 2, 0)
            return carry

        for x in range(2):
            pltpu.matmul_push_rhs(weights(0, 2 * x), 0, x)
        for t in range(STEPS):
            step(0, 0, t, first=True, last=t == STEPS - 1)
        lax.fori_loop(0, 3, pair, 0)
        unit(7, 1)
        finish(7, 1)

    pl.run_scoped(exchange, *[pltpu.ACC(x)((N, 2 * N), f32) for x in (0, 0, 1, 1, 0, 0, 1, 1)])

    def product(*accs):
        for u, (kk, a) in enumerate(UNITS):
            br = bmat(kk, a, 0)
            bi = bmat(kk, a, 1)
            if a:
                br, bi = -br, -bi
            pltpu.matmul_push_rhs(cat0([cat1([br, bi]), cat1([-bi, br])]), a, kk % 2)
            pltpu.matmul_acc_lhs(accs[kk], sig[u], load_staged_rhs=a)
        total = wts[0] * pltpu.matmul_pop(accs[0])
        for kk in range(1, 4):
            total += wts[kk] * pltpu.matmul_pop(accs[kk])
        re = total[:, :N]
        im = total[:, N:]
        back_re = -0.5 * (re + re.T)
        back_im = 0.5 * (im - im.T)
        for o in range(8):
            out[o, 0] = back_im[16 * o:16 * o + 16].astype(bf)
            out[o, 1] = back_re[16 * o:16 * o + 16].astype(bf)

    pl.run_scoped(product, *[pltpu.ACC(kk % 2)((N, 2 * N), f32) for kk in range(4)])


def pack(times, fwd, slab, bsend, f0, f1, here, placed, slices, seen, sems):
    me = lax.axis_index("tm")
    orb = lax.axis_index("orb")
    down = me >> 2
    right = me & 3
    rows_in = pltpu.make_async_copy(slab, here, sems.at[4])
    rows_in.start()
    copies = []
    for half, dst in enumerate((f0, f1)):
        dy, dx = shift(orb, half)
        row = ((((down + dy) & 3) << 2) + ((right + dx) & 3)) << 5
        for r, when in enumerate(matches(times, row, me)):
            spot = 2 * half + r
            copy = pltpu.make_async_copy(fwd.at[:, :, when & 31], slices.at[spot], sems.at[spot])
            copy.start()
            copies.append((copy, pltpu.make_async_copy(slices.at[spot], dst.at[r], sems.at[6 + spot])))
    for e in range(16):
        seen[e] = 0
    rows_in.wait()
    for slot in range(32):
        when = times[(me << 5) + slot]
        holder = when >> 5
        rank = seen[holder]
        seen[holder] = rank + 1
        dy = (down - (holder >> 2)) & 3
        dx = (right - (holder & 3)) & 3
        to = (((dx - dy) & 3) << 1) + (dy >> 1)
        spot = ((dy & 1) << 1) + rank
        for a in range(2):
            for c in range(2):
                placed[to, a, c, spot] = here[a, c, slot]
    for copy, onward in copies:
        copy.wait()
        onward.start()
    rows_out = pltpu.make_async_copy(placed, bsend, sems.at[5])
    rows_out.start()
    for copy, onward in copies:
        onward.wait()
    rows_out.wait()


def on_device(forward, backward_slab, slot_time, pattern, coupling, hamiltonian, lesser_now):
    smem = pl.BlockSpec(memory_space=pltpu.SMEM)
    vmem = pl.BlockSpec(memory_space=pltpu.VMEM)
    hbm = pl.BlockSpec(memory_space=pl.ANY)
    shape = jax.ShapeDtypeStruct
    bsend, f0, f1 = pl.pallas_call(
        pack,
        out_shape=(shape((8, 2, 2, 4, 16, N), bf), shape((2, 2, 2, N, N), bf), shape((2, 2, 2, N, N), bf)),
        in_specs=[smem, hbm, hbm],
        out_specs=(hbm, hbm, hbm),
        scratch_shapes=[pltpu.VMEM((2, 2, 32, 16, N), bf), pltpu.VMEM((8, 2, 2, 4, 16, N), bf),
                        pltpu.VMEM((4, 2, 2, N, N), bf), pltpu.SMEM((16,), jnp.int32),
                        pltpu.SemaphoreType.DMA((10,))],
        compiler_params=pltpu.CompilerParams(vmem_limit_bytes=61 << 20),
    )(slot_time, forward, backward_slab)
    moved = []
    for half, sent in enumerate((f0, f1)):
        pairs = []
        for e in range(16):
            for o in range(8):
                dy, dx = shift(o, half)
                d = ((e // 4 + dy) % 4) * 4 + (e % 4 + dx) % 4
                pairs.append((e * 8 + o, d * 8 + o))
        moved.append(lax.ppermute(sent, ("tm", "orb"), pairs))
    brecv = lax.all_to_all(bsend, "orb", 0, 0, tiled=True)
    V = pltpu.VMEM
    part = pl.pallas_call(
        collide,
        out_shape=shape((8, 2, 16, N), bf),
        in_specs=[smem] + [vmem] * 5,
        out_specs=vmem,
        scratch_shapes=[V((N, N, N), f32), V((N, N), f32), V((8, 2, N, N), f32), V((8, 2, N, N), f32),
                        V((8, N, 2 * N), f32), V((8, N, 2 * N), bf), pltpu.SMEM((4,), f32)],
        compiler_params=pltpu.CompilerParams(vmem_limit_bytes=24 << 20),
    )(slot_time, moved[0], moved[1], brecv, coupling, pattern)
    own = lax.all_to_all(part, "orb", 0, 0, tiled=True).astype(f32).sum(0)
    copies = jnp.broadcast_to(own.astype(bf)[None], (16,) + own.shape)
    spread = lax.all_to_all(copies, "tm", 0, 0, tiled=True).astype(f32)
    start = lax.axis_index("orb") * 16
    high = lax.Precision.HIGHEST
    ham_rows = lax.dynamic_slice_in_dim(hamiltonian, start, 16, 0)
    rows = lax.dynamic_slice_in_dim(lesser_now, start, 16, 1)
    ahead = jnp.dot(ham_rows, jnp.concatenate([lesser_now[0], lesser_now[1]], axis=1), precision=high)
    behind = jnp.dot(rows.reshape(32, N), hamiltonian, precision=high)
    comm_re = ahead[:, :N] - behind[:16]
    comm_im = ahead[:, N:] - behind[16:]
    base = rows + UPDATE_STEP * jnp.stack([comm_im, -comm_re])
    return base + spread.sum(0)


def solution(mesh):
    in_specs = (
        P(None, None, "tm", None, None),
        P(None, None, "tm", "orb", None),
        P(),
        P(),
        P(),
        P(),
        P(),
    )
    return jax.shard_map(on_device, mesh=mesh, in_specs=in_specs, out_specs=P(None, "orb", None), check_vma=False)
```
